512 devices in a mesh: vocab: 64 (over z, x), dp: 8 (over y, core).
Axes of the slice: x: 4, y: 4, z: 16, core: 2. Of those that a mesh axis runs over, the one named last changes fastest.
Arguments:
- hidden_states: bfloat16 [8192, 3584], P(('dp', 'vocab')), parts along dimension 0
- final_gain: float32 [3584], replicated, may hold values from 0.1 to 1.9
- head_weight: bfloat16 [3584, 40960], P(None, 'vocab')
- targets: int32 [8192], P('dp'), parts along dimension 0, may hold values from 0 to 40959
- lengths: int32 [128], P('dp'), parts along dimension 0, may hold values from 1 to 64, 640 in all
- slot_mask: int32 [8192], P(('dp', 'vocab')), parts along dimension 0, may hold values 0 or 1
Outputs:
- logprob: float32 [8192], P(('dp', 'vocab')), parts along dimension 0
- entropy: float32 [8192], P(('dp', 'vocab')), parts along dimension 0
The draws below stay inside these ranges and needn't reach their ends.
There are 8 independent parts, one for each index of `dp`. The reference program is written for one: setup_inputs(seed, part) draws one part's arguments, and reference() takes and returns one part's arrays. A program takes and returns all parts, laid end to end along the dimension named above; an argument that names none is the same for every part. Nothing has to cross between parts.
Inputs may be any that keep to these rules, and one draw needn't show every extreme that they name: Sequence s owns slots s * 64 to (s + 1) * 64 - 1; its first lengths[s] slots are responses, and one sequence fills all 64.
All inputs are finite; a program needn't handle non-finite values. No bound on the sum of `slot_mask` on one device may be relied on, other than what follows from the above.
Results may differ from the reference program's by a relative error of at most 0.0003.
The reference program's roundings to bfloat16 on the way (of `normed`) count: a program that leaves them out, or rounds other values in their place, can miss the bound.
Values may be sent and summed in bfloat16 or wider, within the bound.
No kernel may reach another device: no remote copies, remote signals or barrier semaphores. Data moves between devices by JAX's collectives and lax.ppermute only.
A program may use at most 64 MiB of HBM per device.

```python
import math
import jax
import jax.numpy as jnp
import numpy as np
from jax import lax

D = 3584
SLOT_LEN = 64
VOCAB = 40960
TOKENS = 1024
SEQS = 16


def draw_head_weight(key, part):
    base = jax.random.normal(jax.random.fold_in(key, 101), (D, VOCAB), jnp.float32)
    base = jnp.clip(base, -5.0, 5.0) * (3.0 / math.sqrt(D))
    return base.astype(jnp.bfloat16)


def draw_hidden_states(key, part):
    row_unit = jax.random.uniform(jax.random.fold_in(key, 203), (TOKENS, 1), jnp.float32, 0.0, 1.0)
    col_unit = jax.random.uniform(jax.random.fold_in(key, 205), (1, D), jnp.float32, 0.0, 1.0)
    row_scale = jnp.exp(row_unit * math.log(10.0))
    col_scale = jnp.exp(col_unit * math.log(10.0))
    noise = jnp.clip(jax.random.normal(jax.random.fold_in(key, 201), (TOKENS, D), jnp.float32), -4.0, 4.0)
    field = noise * row_scale * col_scale
    return field.astype(jnp.bfloat16)


def set_ends(values, rng, low, high):
    spot = [jax.random.randint(jax.random.fold_in(rng, axis), (), 0, length) for axis, length in enumerate(values.shape)]
    widest = values.shape.index(max(values.shape))
    next_to = spot[:widest] + [(spot[widest] + 1) % values.shape[widest]] + spot[widest + 1:]
    return values.at[tuple(spot)].set(low).at[tuple(next_to)].set(high)


def rank_table(number_of, slope):
    portions = [(1 << 20) // math.isqrt(rank ** slope) + 1 for rank in range(1, number_of + 1)]
    scale = 1 + sum(portions) // (1 << 30)
    return np.cumsum(np.array([max(1, weight // scale) for weight in portions]))


def ranked(rng, extent, count, lean):
    grid = rank_table(count, lean)
    ticket = jax.random.randint(jax.random.fold_in(rng, 1), extent, 0, int(grid[count - 1]))
    rank = jnp.searchsorted(jnp.asarray(grid, jnp.int32), ticket, side="right")
    return jax.random.permutation(jax.random.fold_in(rng, 2), count)[rank].astype(jnp.int32)


def split_up(count, total, limit, lean):
    loads = [(1 << 20) // math.isqrt(standing ** lean) + 1 for standing in range(2, count + 1)]
    spare, given = total - limit - (count - 1), [1] * (count - 1)
    while spare > 0:
        free = [i for i in range(count - 1) if given[i] < limit]
        pool, budget = sum([loads[i] for i in free]), spare
        for i in free:
            extra = min(limit - given[i], max(1, budget * loads[i] // pool), spare)
            given[i] = given[i] + extra
            spare = spare - extra
    return np.array([limit] + given)


def ragged(stream_key, number_of, total, bound, lean):
    if number_of == 2:
        one = jax.random.randint(stream_key, (), max(1, total - bound), min(bound, total - 1) + 1)
        return jnp.stack([one, total - one])
    tallies = jnp.asarray(split_up(number_of, total, bound, lean), jnp.int32)
    pairs = (number_of - 1) // 2
    giver, taker = tallies[1:1 + 2 * pairs:2], tallies[2:2 + 2 * pairs:2]
    margin = jnp.minimum(giver - 1, bound - taker)
    moved = jax.random.randint(jax.random.fold_in(stream_key, 1), (pairs,), 0, 1 << 20) % (margin + 1)
    tallies = tallies.at[1:1 + 2 * pairs:2].set(giver - moved).at[2:2 + 2 * pairs:2].set(taker + moved)
    return tallies[jax.random.permutation(jax.random.fold_in(stream_key, 2), number_of)]


def setup_inputs(seed: int = 0, part: int = 0) -> dict:
    streams_of = jax.random.split(jax.random.key(seed), 7)
    own_keys = jax.random.split(jax.random.fold_in(streams_of[6], part), 7)
    return {
        "hidden_states": draw_hidden_states(jax.random.fold_in(jax.random.fold_in(streams_of[6], part), 71), part),
        "final_gain": jnp.clip(1.0 + 0.18 * jax.random.normal(streams_of[1], (D,), jnp.float32), 0.1, 1.9),
        "head_weight": draw_head_weight(jax.random.fold_in(streams_of[6], 71), part),
        "targets": set_ends(ranked(own_keys[3], (TOKENS,), VOCAB, 2), jax.random.fold_in(own_keys[3], 3), 0, VOCAB - 1).astype(jnp.int32),
        "lengths": ragged(own_keys[4], SEQS, SEQS * SLOT_LEN * 5 // 8, SLOT_LEN, 2).astype(jnp.int32),
        "slot_mask": set_ends((jax.random.randint(own_keys[5], (TOKENS,), 0, 8) < 7).astype(jnp.int32), jax.random.fold_in(own_keys[5], 1), 0, 1),
    }


def reference(hidden_states, final_gain, head_weight, targets, lengths, slot_mask):
    values = hidden_states.astype(jnp.float32)
    square_mean = lax.optimization_barrier(jnp.mean(values * values, axis=-1, keepdims=True))
    normed = (values * lax.rsqrt(square_mean + 1e-05) * final_gain).astype(jnp.bfloat16)
    blocks = normed.reshape(TOKENS // SLOT_LEN, SLOT_LEN, D)
    wanted = targets.reshape(TOKENS // SLOT_LEN, SLOT_LEN)

    def stats(args):
        rows_block, wanted_block = args
        logits = jnp.dot(rows_block, head_weight, preferred_element_type=jnp.float32)
        highest = lax.optimization_barrier(jnp.max(logits, axis=1))
        shifted = jnp.exp(logits - highest[:, None])
        total = lax.optimization_barrier(jnp.sum(shifted, axis=1))
        weighted = lax.optimization_barrier(jnp.sum(shifted * logits, axis=1))
        chosen = jnp.take_along_axis(logits, wanted_block[:, None].astype(jnp.int32), axis=1)[:, 0]
        return (highest, total, weighted, chosen)
    highest, total, weighted, chosen = lax.map(stats, (blocks, wanted))
    highest = highest.reshape(TOKENS)
    total = total.reshape(TOKENS)
    weighted = weighted.reshape(TOKENS)
    chosen = chosen.reshape(TOKENS)
    slot_index = jnp.arange(TOKENS, dtype=jnp.int32)
    sequence = slot_index // SLOT_LEN
    valid = jnp.logical_and(slot_index % SLOT_LEN < lengths[sequence], slot_mask == 1)
    logprob = jnp.where(valid, chosen - highest - jnp.log(total), jnp.float32(0.0))
    entropy = jnp.where(valid, highest + jnp.log(total) - weighted / total, jnp.float32(0.0))
    return (logprob, entropy)
```

```python
import jax
import jax.numpy as jnp
from jax import lax
from jax.sharding import PartitionSpec as P

SLOT_LEN = 64
RING = 4


def normalize(block, final_gain):
    values = block.astype(jnp.float32)
    square_mean = jnp.mean(values * values, axis=-1, keepdims=True)
    return (values * lax.rsqrt(square_mean + 1e-05) * final_gain).astype(jnp.bfloat16)


def row_stats(normed_rows, head_weight, targets, columns):
    logits = jnp.dot(normed_rows, head_weight, preferred_element_type=jnp.float32)
    highest = jnp.max(logits, axis=1)
    shifted = jnp.exp(logits - highest[:, None])
    total = jnp.sum(shifted, axis=1)
    weighted = jnp.sum(shifted * logits, axis=1)
    chosen = jnp.sum(jnp.where(columns[None, :] == targets[:, None], logits, 0.0), axis=1)
    return jnp.stack([highest, total, weighted, chosen], axis=0)


def gather_rows(normed, n_vocab):
    near = [[z * RING + x for x in range(RING)] for z in range(n_vocab // RING)]
    far = [[z * RING + x for z in range(n_vocab // RING)] for x in range(RING)]
    rows = lax.all_gather(normed, "vocab", axis=0, tiled=True, axis_index_groups=near)
    return lax.all_gather(rows, "vocab", axis=0, tiled=True, axis_index_groups=far)


def exchange(stats, n_vocab):
    own = stats.shape[1] // n_vocab
    sent = stats.reshape(4, n_vocab, own).transpose(1, 0, 2).reshape(n_vocab, 4 * own)
    got = lax.all_to_all(sent, "vocab", 0, 0, tiled=True).reshape(n_vocab, 4, own)
    highest, total, weighted, chosen = got[:, 0], got[:, 1], got[:, 2], got[:, 3]
    peak = jnp.max(highest, axis=0)
    factor = jnp.exp(highest - peak)
    return (
        peak,
        jnp.sum(total * factor, axis=0),
        jnp.sum(weighted * factor, axis=0),
        jnp.sum(chosen, axis=0),
    )


def body(n_vocab, hidden_states, final_gain, head_weight, targets, lengths, slot_mask):
    tok_dev = hidden_states.shape[0]
    v_dev = head_weight.shape[1]
    columns = lax.axis_index("vocab") * v_dev + jnp.arange(v_dev, dtype=jnp.int32)
    normed = normalize(hidden_states, final_gain)
    stats = row_stats(gather_rows(normed, n_vocab), head_weight, targets, columns)
    own_peak, own_total, own_weighted, own_chosen = exchange(stats, n_vocab)
    offset = lax.axis_index("vocab") * tok_dev
    slot_index = offset + jnp.arange(tok_dev, dtype=jnp.int32)
    sequence = slot_index // SLOT_LEN
    seq_ids = jnp.arange(lengths.shape[0], dtype=jnp.int32)
    length_of = jnp.sum(
        jnp.where(sequence[:, None] == seq_ids[None, :], lengths[None, :], 0), axis=1
    )
    valid = jnp.logical_and(slot_index % SLOT_LEN < length_of, slot_mask == 1)
    log_total = jnp.log(own_total)
    logprob = jnp.where(valid, own_chosen - own_peak - log_total, jnp.float32(0.0))
    entropy = jnp.where(valid, own_peak + log_total - own_weighted / own_total, jnp.float32(0.0))
    return (logprob, entropy)


def solution(mesh):
    n_vocab = mesh.shape["vocab"]
    in_specs = (
        P(("dp", "vocab"), None),
        P(),
        P(None, "vocab"),
        P("dp"),
        P("dp"),
        P(("dp", "vocab")),
    )
    out_specs = (P(("dp", "vocab")), P(("dp", "vocab")))

    def run(*args):
        return body(n_vocab, *args)

    return jax.shard_map(run, mesh=mesh, in_specs=in_specs, out_specs=out_specs, check_vma=False)
```

```python
import jax
import jax.numpy as jnp
from jax import lax
from jax.sharding import PartitionSpec as P

SLOT_LEN = 64
RING = 4


def normalize(block, final_gain):
    values = block.astype(jnp.float32)
    square_mean = jnp.mean(values * values, axis=-1, keepdims=True)
    return (values * lax.rsqrt(square_mean + 1e-05) * final_gain).astype(jnp.bfloat16)


def row_stats(normed_rows, head_weight, targets, columns):
    logits = jnp.dot(normed_rows, head_weight, preferred_element_type=jnp.float32)
    highest = jnp.max(logits, axis=1)
    shifted = jnp.exp(logits - highest[:, None])
    total = jnp.sum(shifted, axis=1)
    weighted = jnp.sum(shifted * logits, axis=1)
    chosen = jnp.sum(jnp.where(columns[None, :] == targets[:, None], logits, 0.0), axis=1)
    return jnp.stack([highest, total, weighted, chosen], axis=0)


def ring_steps(n_vocab):
    depth = n_vocab // RING

    def step(block, dz, dx):
        pairs = [
            (z * RING + x, (z + dz) % depth * RING + (x + dx) % RING)
            for z in range(depth)
            for x in range(RING)
        ]
        return lax.ppermute(block, "vocab", pairs)

    return step


def gather_pieces(normed, n_vocab):
    depth = n_vocab // RING
    step = ring_steps(n_vocab)
    same = [[z * RING + x for z in range(p, depth, 2)] for p in range(2) for x in range(RING)]
    here = lax.all_gather(normed, "vocab", axis=0, tiled=True, axis_index_groups=same)
    half = here.shape[0] // 2
    left = step(here, 0, 1)
    right = step(here, 0, -1)
    below = step(here[:half], 1, 0)
    above = step(here[half:], -1, 0)
    far_a = step(left[:half], 0, 1)
    far_b = step(right[half:], 0, -1)
    other = jnp.concatenate([below, above], axis=0)
    other_left = step(other, 0, 1)
    other_right = step(other, 0, -1)
    other_far_a = step(far_a, 1, 0)
    other_far_b = step(far_b, -1, 0)
    return (
        (here, left, right),
        (far_a, far_b, other),
        (other_left, other_right, other_far_a, other_far_b),
    )


ARRIVAL = (0, 3, 1, 2)


def arrange_targets(targets, n_vocab, parity, column):
    depth = n_vocab // RING
    grid = targets.reshape(depth // 2, 2, RING, -1).transpose(1, 2, 0, 3).reshape(2, RING, -1)
    grid = jnp.where(parity == 0, grid, grid[::-1])
    grid = lax.dynamic_slice_in_dim(jnp.concatenate([grid, grid], axis=1), column, RING, axis=1)
    return jnp.stack([grid[:, d] for d in ARRIVAL], axis=1).reshape(-1)


def arrange_stats(stats, n_vocab, parity, column):
    depth = n_vocab // RING
    grid = stats.reshape(4, 2, RING, -1)
    grid = jnp.stack([grid[:, :, ARRIVAL.index(d)] for d in range(RING)], axis=2)
    grid = jnp.where(parity == 0, grid, grid[:, ::-1])
    start = lax.rem(RING - column, RING)
    grid = lax.dynamic_slice_in_dim(jnp.concatenate([grid, grid], axis=2), start, RING, axis=2)
    grid = grid.reshape(4, 2, RING, depth // 2, -1).transpose(3, 1, 2, 0, 4)
    return grid.reshape(n_vocab, -1)


def exchange(sent, n_vocab):
    got = lax.all_to_all(sent, "vocab", 0, 0, tiled=True).reshape(n_vocab, 4, -1)
    highest, total, weighted, chosen = got[:, 0], got[:, 1], got[:, 2], got[:, 3]
    peak = jnp.max(highest, axis=0)
    factor = jnp.exp(highest - peak)
    return (
        peak,
        jnp.sum(total * factor, axis=0),
        jnp.sum(weighted * factor, axis=0),
        jnp.sum(chosen, axis=0),
    )


def validity(lengths, slot_mask, offset):
    slot_index = offset + jnp.arange(slot_mask.shape[0], dtype=jnp.int32)
    sequence = slot_index // SLOT_LEN
    seq_ids = jnp.arange(lengths.shape[0], dtype=jnp.int32)
    length_of = jnp.sum(
        jnp.where(sequence[:, None] == seq_ids[None, :], lengths[None, :], 0), axis=1
    )
    return jnp.logical_and(slot_index % SLOT_LEN < length_of, slot_mask == 1)


def body(n_vocab, hidden_states, final_gain, head_weight, targets, lengths, slot_mask):
    tok_dev = hidden_states.shape[0]
    v_dev = head_weight.shape[1]
    me = lax.axis_index("vocab")
    parity, column = lax.rem(me // RING, 2), lax.rem(me, RING)
    columns = me * v_dev + jnp.arange(v_dev, dtype=jnp.int32)
    normed = normalize(hidden_states, final_gain)
    wanted = arrange_targets(targets, n_vocab, parity, column)
    parts = []
    start = 0
    for pieces in gather_pieces(normed, n_vocab):
        rows = jnp.concatenate(pieces, axis=0)
        parts.append(row_stats(rows, head_weight, wanted[start : start + rows.shape[0]], columns))
        start += rows.shape[0]
    sent = arrange_stats(jnp.concatenate(parts, axis=1), n_vocab, parity, column)
    valid = validity(lengths, slot_mask, me * tok_dev).astype(jnp.int32)
    sent, valid = lax.optimization_barrier((sent, valid))
    own_peak, own_total, own_weighted, own_chosen = exchange(sent, n_vocab)
    valid = valid == 1
    log_total = jnp.log(own_total)
    logprob = jnp.where(valid, own_chosen - own_peak - log_total, jnp.float32(0.0))
    entropy = jnp.where(valid, own_peak + log_total - own_weighted / own_total, jnp.float32(0.0))
    return (logprob, entropy)


def solution(mesh):
    n_vocab = mesh.shape["vocab"]
    in_specs = (
        P(("dp", "vocab"), None),
        P(),
        P(None, "vocab"),
        P("dp"),
        P("dp"),
        P(("dp", "vocab")),
    )
    out_specs = (P(("dp", "vocab")), P(("dp", "vocab")))

    def run(*args):
        return body(n_vocab, *args)

    return jax.shard_map(run, mesh=mesh, in_specs=in_specs, out_specs=out_specs, check_vma=False)
```
